32 devices in a mesh: group: 4 (over y, x), dom: 4 (over z), sub: 2 (over core).
Axes of the slice: x: 2, y: 2, z: 4, core: 2. Of those that a mesh axis runs over, the one named last changes fastest.
Arguments:
- fourier: float32 [1152, 4, 64, 16], P('dom', None, ('group', 'sub')), may hold values from -6 to 6
- legendre: float32 [8, 1152, 640], P('dom'), may hold values from -0.1875 to 0.1875
- eta_start: float32 [128, 512], P(('group', 'sub'), 'dom'), may hold values from -6 to 6
- coefs: float32 [9, 128, 512], P(None, ('group', 'sub'), 'dom'), may hold values from 0.1 to 1
- wet: int32 [128, 512], P(('group', 'sub'), 'dom'), may hold values 0 or 1
- src_index: int32 [128, 4, 2], P(('group', 'sub'), 'dom'), may hold values from 0 to 143
- regrid_weight: float32 [128, 4, 2, 128, 128], P(('group', 'sub'), 'dom'), may hold values from -0.375 to 0.375
Outputs:
- spectral: float32 [8, 4, 64, 2, 640], P('dom', None, ('group', 'sub'))
- eta_final: float32 [128, 512], P(('group', 'sub'), 'dom')
The draws below stay inside these ranges and needn't reach their ends.
All inputs are finite; a program needn't handle non-finite values. No bound on the sum of `wet` on one device may be relied on, other than what follows from the above.
Results may differ from the reference program's by a relative error of at most 0.00011.
Values sent between devices are 32-bit elements; how exact they have to be, the bound alone decides.
A program may use at most 64 MiB of HBM per device.

```python
import math
import jax
import jax.numpy as jnp
from jax import lax

LAT = 1152
NDEG = 640
VARS = 4
LEV_DEV = 8
ROWS_DEV = 16
BLK = 128
KSRC = 2
SUBS = 8
M = 8
LEV = 64
BANDS = 8
SRC_ALL = 144
OROWS = 128
OCOLS = 512
N_DOM = 4


def touch_ends(values, stream_key, low, top_value):
    longest = values.shape.index(max(values.shape))
    spots = []
    for shift in (0, 1):
        where = [jax.random.randint(jax.random.fold_in(stream_key, axis), (), 0, length) for axis, length in enumerate(values.shape)]
        where[longest] = (where[longest] + shift) % values.shape[longest]
        spots.append(tuple(where))
    return values.at[spots[0]].set(low).at[spots[1]].set(top_value)


def shard_levels(own_key, shape, pieces, smallest, high):
    factor_of = 1.0
    for axis_at, blocks in pieces:
        heights = jax.random.uniform(jax.random.fold_in(jax.random.fold_in(own_key, 6), axis_at), (blocks,), jnp.float32, smallest / len(pieces), high / len(pieces))
        factor_of = factor_of * jnp.repeat(jnp.exp(heights), shape[axis_at] // blocks).reshape((-1,) + (1,) * (len(shape) - 1 - axis_at))
    return factor_of


def scatter_about(stream_key, extent, deviation, reach, cuts=(), kind=jnp.bfloat16):
    level = shard_levels(stream_key, extent, cuts, -0.22, 0.18) if cuts else 1.0
    result = jax.random.normal(stream_key, extent, jnp.float32) * deviation * level
    return jnp.minimum(jnp.maximum(result, -reach), reach).astype(kind)


def setup_inputs(seed: int = 0) -> dict:
    streams_of = jax.random.split(jax.random.key(seed), 8)
    fourier = scatter_about(streams_of[0], (LAT, VARS, LEV, 2 * M), 1.0, 6.0, ((0, 4), (2, 8)), jnp.float32)
    legendre = scatter_about(streams_of[1], (M, LAT, NDEG), LAT ** -0.5, 0.1875, ((0, 4),), jnp.float32)
    eta_start = scatter_about(streams_of[2], (OROWS, OCOLS), 1.0, 6.0, ((0, 8), (1, 4)), jnp.float32)
    coefs = jnp.clip(jnp.exp(math.log(1.0) - 2.3025851 * jax.random.uniform(streams_of[3], (9, OROWS, OCOLS), jnp.float32) ** shard_levels(streams_of[3], (9, OROWS, OCOLS), ((1, 8), (2, 4)), -0.2, 0.2)), 0.1, 1.0)
    wet = touch_ends((jax.random.randint(streams_of[4], (OROWS, OCOLS), 0, 8) < 7).astype(jnp.int32), jax.random.fold_in(streams_of[4], 1), 0, 1)
    src_index = touch_ends(jax.random.randint(streams_of[5], (OROWS, N_DOM, KSRC), 0, SRC_ALL), jax.random.fold_in(streams_of[5], 1), 0, SRC_ALL - 1).astype(jnp.int32)
    regrid_weight = scatter_about(streams_of[6], (OROWS, N_DOM, KSRC, BLK, BLK), (BLK * KSRC) ** -0.5, 0.375, ((0, 8), (1, 4)), jnp.float32)
    return dict(fourier=fourier, legendre=legendre, eta_start=eta_start, coefs=coefs, wet=wet, src_index=src_index, regrid_weight=regrid_weight)


forcing_rate = 0.5


def reference(fourier, legendre, eta_start, coefs, wet, src_index, regrid_weight):
    parts = fourier.reshape(LAT, VARS, LEV, M, 2)
    spectral = jnp.einsum('man,avlmr->mvlrn', legendre, parts, precision=lax.Precision.HIGHEST)
    surface = fourier[:, 0, ::LEV_DEV, :]
    flux = jnp.transpose(surface, (1, 0, 2)).reshape(BANDS, SRC_ALL, BLK)
    band = (jnp.arange(OROWS) // ROWS_DEV).astype(jnp.int32)
    picked = flux[band[:, None, None], src_index]
    forcing = jnp.einsum('rdkts,rdks->rdt', regrid_weight, picked, precision=lax.Precision.HIGHEST)
    forcing = forcing.reshape(OROWS, OCOLS)
    norm = coefs / jnp.sum(coefs, axis=0)
    wetness = wet.astype(jnp.float32)
    eta = eta_start
    for cycle in range(SUBS):
        padded = jnp.pad(eta, 1)
        total = norm[0] * padded[0:OROWS, 0:OCOLS]
        for index in range(1, 9):
            shift_row = index // 3
            shift_col = index % 3
            total = total + norm[index] * padded[shift_row:shift_row + OROWS, shift_col:shift_col + OCOLS]
        eta = wetness * (total + forcing_rate * forcing)
    return spectral, eta
```

```python
import functools

import jax
import jax.numpy as jnp
from jax import lax
from jax.experimental import pallas as pl
from jax.experimental.pallas import tpu as pltpu
from jax.sharding import PartitionSpec as P

SUBS = 8
RATE = 0.5
MESH = pl.DeviceIdType.MESH
F32 = jnp.float32
BF16 = jnp.bfloat16


def split(x):
    high = x.astype(BF16)
    return high, (x - high.astype(F32)).astype(BF16)


def dot(a, b):
    return jnp.dot(a, b, preferred_element_type=F32)


def kernel(
    dims,
    x_hbm, l_hbm, eta_hbm, coef_hbm, wet_hbm, idx, w_hbm, fl_hbm,
    spec, eta_out,
    xv, xr, lv, wv, flb, sb, rb, lh, ll, th, tl, xt, cx, wx, ex, fx, fl_w, fl_e, pk_w, pk_e, h_w, h_e, nrm,
    lsem, ssem, rsem,
):
    n, rows_n, subs_n, la, pairs, cols, lev, m_dev, rows, count, slot = dims
    width = SUBS
    main = la // 128 * 128
    tail = la - main
    tiles = main // 128
    cdev = 2 * m_dev
    pad = flb.shape[0] // n
    me = lax.axis_index("dom")
    row = lax.axis_index("group") * subs_n + lax.axis_index("sub")

    def at(drow, ddom):
        target = {}
        if drow:
            other = lax.rem(row + rows_n + drow, rows_n)
            target["group"] = other // subs_n
            target["sub"] = lax.rem(other, subs_n)
        if ddom:
            target["dom"] = lax.rem(me + n + ddom, n)
        return target

    locals_ = []

    def fetch(src, dst):
        copy = pltpu.make_async_copy(src, dst, lsem.at[len(locals_)])
        locals_.append(copy)
        copy.start()
        return copy

    remotes = []

    def send(src, dst, target):
        i = len(remotes)
        copy = pltpu.make_async_remote_copy(
            src_ref=src, dst_ref=dst, send_sem=ssem.at[i], recv_sem=rsem.at[i],
            device_id=target, device_id_type=MESH,
        )
        remotes.append(copy)
        copy.start()
        return copy

    barrier = pltpu.get_barrier_semaphore()
    greet = [at(0, r) for r in range(1, n)]
    greet += [at(dr, dd) for dr in (-1, 1) for dd in (-1, 0, 1)]
    for target in greet:
        pl.semaphore_signal(barrier, inc=1, device_id=target, device_id_type=MESH)
    get_c = fetch(coef_hbm, cx.at[:, pl.ds(width, rows), :])
    get_w = fetch(wet_hbm, wx.at[pl.ds(width, rows), :])
    get_e = fetch(eta_hbm, ex.at[pl.ds(width, rows), :])
    get_x = [fetch(x_hbm.at[:, pl.ds(t * 128, 128)], xv.at[t]) for t in range(tiles)]
    if tail:
        get_x.append(fetch(x_hbm.at[:, pl.ds(main, tail)], xr))
    mine = pl.ds(pl.multiple_of(me * pad, 8), pad)
    get_f = fetch(fl_hbm, flb.at[mine, :])
    get_r = fetch(w_hbm, wv)
    get_l = [fetch(l_hbm.at[m], lv.at[m]) for m in range(m_dev)]

    lane = lax.broadcasted_iota(jnp.int32, (1, 128), 1)
    get_c.wait()
    get_w.wait()
    get_e.wait()
    own = pl.ds(width, rows)
    planes = [cx[k, own, :] for k in range(9)] + [wx[own, :].astype(F32), ex[own, :]]
    left = jnp.zeros((rows, 128), F32)
    right = jnp.zeros((rows, 128), F32)
    for p, plane in enumerate(planes):
        here = (lane >= width * p) & (lane < width * (p + 1))
        left = jnp.where(here, pltpu.roll(plane, width * p, 1), left)
        right = jnp.where(here, pltpu.roll(plane, (width * p + width) % 128, 1), right)
    pk_w[...] = left
    pk_e[...] = right

    pl.semaphore_wait(barrier, len(greet))
    top, bottom = pl.ds(0, width), pl.ds(rows - width, width)
    halo_n, halo_s = pl.ds(0, width), pl.ds(width + rows, width)
    get_flux = [send(fl_hbm, flb.at[mine, :], at(0, r)) for r in range(1, n)]
    edges = []
    for src, dst in ((coef_hbm, cx), ):
        edges.append(send(src.at[:, bottom, :], dst.at[:, halo_n, :], at(1, 0)))
        edges.append(send(src.at[:, top, :], dst.at[:, halo_s, :], at(-1, 0)))
    for src, dst in ((wet_hbm, wx), (eta_hbm, ex)):
        edges.append(send(src.at[bottom, :], dst.at[halo_n, :], at(1, 0)))
        edges.append(send(src.at[top, :], dst.at[halo_s, :], at(-1, 0)))
    for src, dst, dd in ((pk_e, h_w, 1), (pk_w, h_e, -1)):
        edges.append(send(src, dst.at[own, :], at(0, dd)))
        edges.append(send(src.at[bottom, :], dst.at[halo_n, :], at(1, dd)))
        edges.append(send(src.at[top, :], dst.at[halo_s, :], at(-1, dd)))

    for copy in get_x:
        copy.wait()
    vars_n = pairs // lev
    if tail:
        xv[tiles] = jnp.concatenate([xr[...], jnp.zeros((xr.shape[0], 128 - tail), F32)], axis=1)

    def pack(dest, store):
        for c in range(cdev):
            where = dest * cdev + c
            for t in range(tiles):
                store(
                    t * cdev * pairs + c * pairs, pairs,
                    xv.at[t][pl.ds(where, pairs, stride=cols), :],
                )
            if tail:
                rest = xv.at[tiles][pl.ds(where, pairs, stride=cols), :]
                total = rest[0:lev]
                for v in range(1, vars_n):
                    total = total + pltpu.roll(rest[v * lev:(v + 1) * lev], slot * v, 1)
                store(tiles * cdev * pairs + c * lev, lev, total)

    def keep(buffer, which):
        def store(first, height, value):
            buffer[which, pl.ds(first, height), :] = value
        return store

    blocks = []
    for r in range(1, n):
        dest = lax.rem(me + r, n)
        pack(dest, keep(sb, r - 1))
        blocks.append(send(sb.at[r - 1], rb.at[me], at(0, r)))
    pack(me, keep(rb, me))

    for copy in get_l:
        copy.wait()
    per = 128 // slot

    def split_legendre(d, carry):
        for m in range(m_dev):
            if main:
                h, l = split(lv[m, pl.ds(pl.multiple_of(d * la, 8), main), :])
                lh[m, d] = h
                ll[m, d] = l
            if tail:
                part = lv[m, pl.ds(pl.multiple_of(d * la + main, 8), tail), :]
                if slot > tail:
                    part = jnp.concatenate([part, jnp.zeros((slot - tail, part.shape[1]), F32)], axis=0)
                h, l = split(part)
                th[m, d] = h
                tl[m, d] = l
        return carry

    lax.fori_loop(0, n, split_legendre, 0)

    get_f.wait()
    for copy in get_flux:
        copy.wait_recv()
    get_r.wait()

    def regrid(i, total):
        part = None
        for k in range(2):
            block = idx[k, i]
            at_row = (block // count) * pad + lax.rem(block, count)
            term = wv[i, k] * flb[pl.ds(at_row, 1), :]
            part = term if part is None else part + term
        return jnp.where(lane == i, jnp.sum(part, axis=1, keepdims=True), total)

    forced = lax.fori_loop(0, rows, regrid, jnp.zeros((128, 128), F32))
    fx[own, :] = forced.T[0:rows]
    up, down = pl.ds(width, width), pl.ds(rows, width)
    force = []
    force.append(send(fx.at[down, :], fx.at[halo_n, :], at(1, 0)))
    force.append(send(fx.at[up, :], fx.at[halo_s, :], at(-1, 0)))
    for dst, dd in ((fl_w, 1), (fl_e, -1)):
        force.append(send(fx.at[own, :], dst.at[own, :], at(0, dd)))
        force.append(send(fx.at[down, :], dst.at[halo_n, :], at(1, dd)))
        force.append(send(fx.at[up, :], dst.at[halo_s, :], at(-1, dd)))

    for copy in edges:
        copy.wait_recv()
    tall = rows + 2 * width
    spot = lax.broadcasted_iota(jnp.int32, (tall, 128), 0) + row * rows - width
    lanes = lax.broadcasted_iota(jnp.int32, (tall, 128), 1)
    inside = (spot >= 0) & (spot < rows_n * rows)
    is_e = lanes < width
    is_w = lanes >= 128 - width
    side_in = inside & ((is_e & (me < n - 1)) | (is_w & (me > 0)))
    west, east = h_w[...], h_e[...]

    def side(p):
        from_e = pltpu.roll(east, (128 - width * p) % 128, 1)
        from_w = pltpu.roll(west, (256 - width - width * p) % 128, 1)
        return jnp.where(is_e, from_e, from_w)

    def extend(middle, p, other):
        return (
            jnp.where(inside, middle, other),
            jnp.where(side_in, side(p), other),
        )

    coefs = [extend(cx[k], k, 1.0) for k in range(9)]
    mask = extend(wx[...].astype(F32), 9, 0.0)
    eta2 = extend(ex[...], 10, 0.0)
    for h in range(2):
        scale = mask[h] / functools.reduce(lambda a, b: a + b, [c[h] for c in coefs])
        for k in range(9):
            nrm[k, :, h * 128:(h + 1) * 128] = coefs[k][h] * scale

    half = 2 * pairs

    def contract(d, first):
        for m in range(m_dev):
            if main:
                parts = [
                    rb[d, pl.ds(t * cdev * pairs + m * half, half), :] for t in range(tiles)
                ]
                h, l = split(jnp.concatenate(parts, axis=1) if tiles > 1 else parts[0])
                value = dot(h, lh[m, d]) + dot(h, ll[m, d]) + dot(l, lh[m, d])
                if first:
                    spec[m] = value
                else:
                    spec[m] += value
            elif first:
                spec[m] = jnp.zeros_like(spec[m])
        if tail:
            e = lax.rem(d, per)
            chunk = d // per
            for c in range(cdev):
                packed = rb[d, pl.ds(tiles * cdev * pairs + c * lev, lev), :]
                for v in range(vars_n):
                    turn = lax.rem((e - v) * slot + 128 * vars_n, 128)
                    moved = pltpu.roll(packed, turn, 1)
                    place = pl.ds(c * pairs + v * lev, lev)
                    here = (lane >= e * slot) & (lane < (e + 1) * slot)
                    xt[chunk, place, :] = jnp.where(here, moved, xt[chunk, place, :])

    if tail:
        xt[...] = jnp.zeros_like(xt)
    contract(me, True)

    for copy in force:
        copy.wait_recv()
    live = jnp.concatenate([mask[0], mask[1]], axis=1)
    sides = jnp.where(side_in, jnp.where(is_e, fl_e[...], fl_w[...]), 0.0)
    pull = live * (RATE * jnp.concatenate([jnp.where(inside, fx[...], 0.0), sides], axis=1))
    eta = jnp.concatenate([eta2[0], eta2[1]], axis=1)
    for step in range(SUBS):
        across = [pltpu.roll(eta, 1, 1), eta, pltpu.roll(eta, 255, 1)]
        total = pull
        for q in range(3):
            turned = [pltpu.roll(across[q], 1, 0), across[q], pltpu.roll(across[q], tall - 1, 0)]
            for p in range(3):
                total = total + nrm[3 * p + q] * turned[p]
        eta = total
    eta_out[...] = eta[width:width + rows, 0:128]

    for r in range(1, n):
        blocks[r - 1].wait_recv()
        contract(lax.rem(me + n - r, n), False)
    if tail:
        for chunk in range(xt.shape[0]):
            for m in range(m_dev):
                h, l = split(xt[chunk, m * half:(m + 1) * half, :])
                group = pl.ds(chunk * per, per)
                high = th[m, group].reshape(128, th.shape[-1])
                low = tl[m, group].reshape(128, tl.shape[-1])
                spec[m] += dot(h, high) + dot(h, low) + dot(l, high)
    for copy in remotes:
        copy.wait_send()


def body(fourier, legendre, eta_start, coefs, wet, src_index, regrid_weight):
    n = lax.axis_size("dom")
    subs_n = lax.axis_size("sub")
    rows_n = lax.axis_size("group") * subs_n
    la, vars_n, lev, cols = fourier.shape
    m_dev, lat, ndeg = legendre.shape
    rows, blk = eta_start.shape
    pairs = vars_n * lev
    main = la // 128 * 128
    tail = la - main
    slot = -(-tail // 16) * 16 if tail else 128
    while 128 % slot:
        slot += 16
    if tail:
        assert slot * vars_n <= 128 and n % (128 // slot) == 0
    chunks = max(1, n // (128 // slot))
    surface = fourier[:, 0, 0, :]
    count = la * cols // blk
    flux = surface.reshape(count, blk)
    pad = -(-count // 8) * 8
    flux = jnp.pad(flux, ((0, pad - count), (0, 0)))
    x = jnp.transpose(fourier, (1, 2, 3, 0)).reshape(pairs * cols, la)
    index = jnp.transpose(src_index.reshape(rows, 2), (1, 0))
    weight = regrid_weight.reshape(rows, 2, blk, blk)
    depth = main // 128 * 2 * m_dev * pairs + (2 * m_dev * lev if tail else 0)
    tall = rows + 2 * SUBS
    dims = (n, rows_n, subs_n, la, pairs, cols, lev, m_dev, rows, count, slot)
    sends = (n - 1) * 2 + 12 + 8
    any_ = pl.BlockSpec(memory_space=pl.ANY)
    vmem = pl.BlockSpec(memory_space=pltpu.VMEM)
    spec, eta = pl.pallas_call(
        functools.partial(kernel, dims),
        out_shape=(
            jax.ShapeDtypeStruct((m_dev, 2 * pairs, ndeg), F32),
            jax.ShapeDtypeStruct((rows, blk), F32),
        ),
        in_specs=[any_] * 5 + [pl.BlockSpec(memory_space=pltpu.SMEM)] + [any_] * 2,
        out_specs=(vmem, vmem),
        scratch_shapes=[
            pltpu.VMEM((-(-la // 128), pairs * cols, 128), F32),
            pltpu.VMEM((pairs * cols, max(tail, 8)), F32),
            pltpu.VMEM(legendre.shape, F32),
            pltpu.VMEM(weight.shape, F32),
            pltpu.VMEM((n * pad, blk), F32),
            pltpu.VMEM((n - 1, depth, 128), F32),
            pltpu.VMEM((n, depth, 128), F32),
            pltpu.VMEM((m_dev, n, max(main, 16), ndeg), BF16),
            pltpu.VMEM((m_dev, n, max(main, 16), ndeg), BF16),
            pltpu.VMEM((m_dev, n, slot, ndeg), BF16),
            pltpu.VMEM((m_dev, n, slot, ndeg), BF16),
            pltpu.VMEM((chunks, 2 * m_dev * pairs, 128), F32),
            pltpu.VMEM((9, tall, blk), F32),
            pltpu.VMEM((tall, blk), jnp.int32),
            pltpu.VMEM((tall, blk), F32),
            pltpu.VMEM((tall, blk), F32),
            pltpu.VMEM((tall, blk), F32),
            pltpu.VMEM((tall, blk), F32),
            pltpu.VMEM((rows, blk), F32),
            pltpu.VMEM((rows, blk), F32),
            pltpu.VMEM((tall, blk), F32),
            pltpu.VMEM((tall, blk), F32),
            pltpu.VMEM((9, tall, 2 * blk), F32),
            pltpu.SemaphoreType.DMA((8 + main // 128 + m_dev,)),
            pltpu.SemaphoreType.DMA((sends,)),
            pltpu.SemaphoreType.DMA((sends,)),
        ],
        compiler_params=pltpu.CompilerParams(collective_id=0, has_side_effects=True),
    )(x, legendre, eta_start, coefs, wet, index, weight, flux)
    spectral = spec.reshape(m_dev, 2, vars_n, lev, ndeg)
    return jnp.transpose(spectral, (0, 2, 3, 1, 4)), eta


def solution(mesh):
    placed = (
        P("dom", None, ("group", "sub"), None),
        P("dom", None, None),
        P(("group", "sub"), "dom"),
        P(None, ("group", "sub"), "dom"),
        P(("group", "sub"), "dom"),
        P(("group", "sub"), "dom", None),
        P(("group", "sub"), "dom", None, None, None),
    )
    return jax.shard_map(
        body,
        mesh=mesh,
        in_specs=placed,
        out_specs=(P("dom", None, ("group", "sub"), None, None), P(("group", "sub"), "dom")),
        check_vma=False,
    )
```

```python
import functools

import jax
import jax.numpy as jnp
from jax import lax
from jax.experimental import pallas as pl
from jax.experimental.pallas import tpu as pltpu
from jax.sharding import PartitionSpec as P

SUBS = 8
RATE = 0.5
MESH = pl.DeviceIdType.MESH
F32 = jnp.float32
BF16 = jnp.bfloat16


def split(x):
    high = x.astype(BF16)
    return high, (x - high.astype(F32)).astype(BF16)


def dot(a, b):
    return jnp.dot(a, b, preferred_element_type=F32)


def kernel(
    dims,
    *refs,
):
    x_hbm, l_hbm, eta_hbm, coef_hbm, wet_hbm, idx_hbm, w_hbm = refs[:7]
    fl_hbm = refs[7] if dims[-1] else None
    (
    out, eta_out,
    idx, acc, tr, xv, xr, lv, wv, flb, sb, rb, lh, ll, th, tl, xt, cx, wx, ex, fx, fl_w, fl_e, pk_w, pk_e, h_w, h_e, nrm,
    lsem, ssem, rsem,
    ) = refs[7 + dims[-1]:]
    n, rows_n, subs_n, la, pairs, cols, lev, m_dev, rows, count, slot, given = dims
    width = SUBS
    main = la // 128 * 128
    tail = la - main
    tiles = main // 128
    cdev = 2 * m_dev
    pad = flb.shape[0] // n
    me = lax.axis_index("dom")
    row = lax.axis_index("group") * subs_n + lax.axis_index("sub")

    def at(drow, ddom):
        target = {}
        if drow:
            other = lax.rem(row + rows_n + drow, rows_n)
            target["group"] = other // subs_n
            target["sub"] = lax.rem(other, subs_n)
        if ddom:
            target["dom"] = lax.rem(me + n + ddom, n)
        return target

    locals_ = []

    def fetch(src, dst):
        copy = pltpu.make_async_copy(src, dst, lsem.at[len(locals_)])
        locals_.append(copy)
        copy.start()
        return copy

    remotes = []

    def send(src, dst, target, ddom=0):
        i = len(remotes)
        copy = pltpu.make_async_remote_copy(
            src_ref=src, dst_ref=dst, send_sem=ssem.at[i], recv_sem=rsem.at[i],
            device_id=target, device_id_type=MESH,
        )
        go = {1: me < n - 1, -1: me > 0}.get(ddom)
        come = {1: me > 0, -1: me < n - 1}.get(ddom)
        remotes.append((copy, go))
        if go is None:
            copy.start()
        else:
            pl.when(go)(copy.start)
        return copy, come

    def arrive(sent):
        copy, come = sent
        if come is None:
            copy.wait_recv()
        else:
            pl.when(come)(copy.wait_recv)

    def partner(r):
        if n & (n - 1):
            return lax.rem(me + r, n), lax.rem(me + n - r, n)
        other = me
        bit = 1
        while bit < n:
            if r & bit:
                other = other + bit - 2 * bit * lax.rem(me // bit, 2)
            bit *= 2
        return other, other

    barrier = pltpu.get_barrier_semaphore()
    greet = [at(0, r) for r in range(1, n)]
    greet += [at(dr, dd) for dr in (-1, 1) for dd in (-1, 0, 1)]
    for target in greet:
        pl.semaphore_signal(barrier, inc=1, device_id=target, device_id_type=MESH)
    get_c = fetch(coef_hbm, cx.at[:, pl.ds(width, rows), :])
    get_w = fetch(wet_hbm, wx.at[pl.ds(width, rows), :])
    get_e = fetch(eta_hbm, ex.at[pl.ds(width, rows), :])
    get_x = [fetch(x_hbm.at[:, pl.ds(t * 128, 128)], xv.at[t]) for t in range(tiles)]
    if tail:
        get_x.append(fetch(x_hbm.at[:, pl.ds(main, tail)], xr))
    mine = pl.ds(pl.multiple_of(me * pad, 8), pad)
    get_f = fetch(fl_hbm, flb.at[mine, :]) if given else None
    get_r = [fetch(idx_hbm, idx), fetch(w_hbm, wv)]
    get_l = [fetch(l_hbm.at[m], lv.at[m]) for m in range(m_dev)]

    lane = lax.broadcasted_iota(jnp.int32, (1, 128), 1)
    get_c.wait()
    get_w.wait()
    get_e.wait()
    own = pl.ds(width, rows)
    planes = [cx[k, own, :] for k in range(9)] + [wx[own, :].astype(F32), ex[own, :]]
    left = jnp.zeros((rows, 128), F32)
    right = jnp.zeros((rows, 128), F32)
    for p, plane in enumerate(planes):
        here = (lane >= width * p) & (lane < width * (p + 1))
        left = jnp.where(here, pltpu.roll(plane, width * p, 1), left)
        right = jnp.where(here, pltpu.roll(plane, (width * p + width) % 128, 1), right)
    pk_w[...] = left
    pk_e[...] = right

    for copy in get_x:
        copy.wait()
    vars_n = pairs // lev
    if tail:
        xv[tiles] = jnp.concatenate([xr[...], jnp.zeros((xr.shape[0], 128 - tail), F32)], axis=1)
    if given:
        get_f.wait()
    else:
        group = 128 // cols
        for t in range(xv.shape[0]):
            plane = jnp.concatenate([xv[t, 0:cols, :], jnp.zeros((128 - cols, 128), F32)], axis=0)
            tr[t * 128:(t + 1) * 128, :] = plane.T
        flux = tr[pl.ds(0, pad, stride=group), :]
        for g in range(1, group):
            flux = flux + pltpu.roll(tr[pl.ds(g, pad, stride=group), :], cols * g, 1)
        flb[mine, :] = flux

    def pack(dest, store):
        for c in range(cdev):
            where = dest * cdev + c
            for t in range(tiles):
                store(
                    t * cdev * pairs + c * pairs, pairs,
                    xv.at[t][pl.ds(where, pairs, stride=cols), :],
                )
            if tail:
                rest = xv.at[tiles][pl.ds(where, pairs, stride=cols), :]
                total = rest[0:lev]
                for v in range(1, vars_n):
                    total = total + pltpu.roll(rest[v * lev:(v + 1) * lev], slot * v, 1)
                store(tiles * cdev * pairs + c * lev, lev, total)

    def keep(buffer, which):
        def store(first, height, value):
            buffer[which, pl.ds(first, height), :] = value
        return store

    order = sorted(range(1, n), key=lambda r: (r < n // 2, r))
    for r in order:
        pack(partner(r)[0], keep(sb, r - 1))
    pack(me, keep(rb, me))
    blocks = {}

    def send_block(r):
        blocks[r] = send(sb.at[r - 1], rb.at[me], at_dom(partner(r)[0]))

    def at_dom(other):
        return {"dom": other}

    pl.semaphore_wait(barrier, len(greet))
    top, bottom = pl.ds(0, width), pl.ds(rows - width, width)
    halo_n, halo_s = pl.ds(0, width), pl.ds(width + rows, width)
    get_flux = [send(flb.at[mine, :], flb.at[mine, :], at_dom(partner(r)[0])) for r in order]
    edges = []
    for src, dst in ((coef_hbm, cx), ):
        edges.append(send(src.at[:, bottom, :], dst.at[:, halo_n, :], at(1, 0)))
        edges.append(send(src.at[:, top, :], dst.at[:, halo_s, :], at(-1, 0)))
    for src, dst in ((wet_hbm, wx), (eta_hbm, ex)):
        edges.append(send(src.at[bottom, :], dst.at[halo_n, :], at(1, 0)))
        edges.append(send(src.at[top, :], dst.at[halo_s, :], at(-1, 0)))
    for src, dst, dd in ((pk_e, h_w, 1), (pk_w, h_e, -1)):
        edges.append(send(src, dst.at[own, :], at(0, dd), dd))
        edges.append(send(src.at[bottom, :], dst.at[halo_n, :], at(1, dd), dd))
        edges.append(send(src.at[top, :], dst.at[halo_s, :], at(-1, dd), dd))

    send_block(order[0])

    for copy in get_l:
        copy.wait()
    per = 128 // slot

    def split_legendre(d, carry):
        for m in range(m_dev):
            if main:
                h, l = split(lv[m, pl.ds(pl.multiple_of(d * la, 8), main), :])
                lh[m, d] = h
                ll[m, d] = l
            if tail:
                part = lv[m, pl.ds(pl.multiple_of(d * la + main, 8), tail), :]
                if slot > tail:
                    part = jnp.concatenate([part, jnp.zeros((slot - tail, part.shape[1]), F32)], axis=0)
                h, l = split(part)
                th[m, d] = h
                tl[m, d] = l
        return carry

    lax.fori_loop(0, n, split_legendre, 0)

    for copy in get_flux:
        arrive(copy)
    for copy in get_r:
        copy.wait()

    def regrid(i, total):
        part = None
        for k in range(2):
            block = idx[k, i]
            at_row = (block // count) * pad + lax.rem(block, count)
            term = wv[i, k] * flb[pl.ds(at_row, 1), :]
            part = term if part is None else part + term
        return jnp.where(lane == i, jnp.sum(part, axis=1, keepdims=True), total)

    forced = lax.fori_loop(0, rows, regrid, jnp.zeros((128, 128), F32))
    fx[own, :] = forced.T[0:rows]
    up, down = pl.ds(width, width), pl.ds(rows, width)
    force = []
    force.append(send(fx.at[down, :], fx.at[halo_n, :], at(1, 0)))
    force.append(send(fx.at[up, :], fx.at[halo_s, :], at(-1, 0)))
    for dst, dd in ((fl_w, 1), (fl_e, -1)):
        force.append(send(fx.at[own, :], dst.at[own, :], at(0, dd), dd))
        force.append(send(fx.at[down, :], dst.at[halo_n, :], at(1, dd), dd))
        force.append(send(fx.at[up, :], dst.at[halo_s, :], at(-1, dd), dd))

    for r in order[1:]:
        send_block(r)

    for copy in edges:
        arrive(copy)
    tall = rows + 2 * width
    spot = lax.broadcasted_iota(jnp.int32, (tall, 128), 0) + row * rows - width
    lanes = lax.broadcasted_iota(jnp.int32, (tall, 128), 1)
    inside = (spot >= 0) & (spot < rows_n * rows)
    is_e = lanes < width
    is_w = lanes >= 128 - width
    side_in = inside & ((is_e & (me < n - 1)) | (is_w & (me > 0)))
    west, east = h_w[...], h_e[...]

    def side(p):
        from_e = pltpu.roll(east, (128 - width * p) % 128, 1)
        from_w = pltpu.roll(west, (256 - width - width * p) % 128, 1)
        return jnp.where(is_e, from_e, from_w)

    def extend(middle, p, other):
        return (
            jnp.where(inside, middle, other),
            jnp.where(side_in, side(p), other),
        )

    coefs = [extend(cx[k], k, 1.0) for k in range(9)]
    mask = extend(wx[...].astype(F32), 9, 0.0)
    eta2 = extend(ex[...], 10, 0.0)
    for h in range(2):
        scale = mask[h] / functools.reduce(lambda a, b: a + b, [c[h] for c in coefs])
        for k in range(9):
            nrm[k, :, h * 128:(h + 1) * 128] = coefs[k][h] * scale

    half = 2 * pairs

    def contract(d, first):
        for m in range(m_dev):
            if main:
                parts = [
                    rb[d, pl.ds(t * cdev * pairs + m * half, half), :] for t in range(tiles)
                ]
                h, l = split(jnp.concatenate(parts, axis=1) if tiles > 1 else parts[0])
                value = dot(h, lh[m, d]) + dot(h, ll[m, d]) + dot(l, lh[m, d])
                if first:
                    acc[m] = value
                else:
                    acc[m] += value
            elif first:
                acc[m] = jnp.zeros_like(acc[m])
        if tail:
            e = lax.rem(d, per)
            chunk = d // per
            for c in range(cdev):
                packed = rb[d, pl.ds(tiles * cdev * pairs + c * lev, lev), :]
                for v in range(vars_n):
                    turn = lax.rem((e - v) * slot + 128 * vars_n, 128)
                    moved = pltpu.roll(packed, turn, 1)
                    place = pl.ds(c * pairs + v * lev, lev)
                    here = (lane >= e * slot) & (lane < (e + 1) * slot)
                    xt[chunk, place, :] = jnp.where(here, moved, xt[chunk, place, :])

    if tail:
        xt[...] = jnp.zeros_like(xt)
    contract(me, True)

    for copy in force:
        arrive(copy)
    live = jnp.concatenate([mask[0], mask[1]], axis=1)
    sides = jnp.where(side_in, jnp.where(is_e, fl_e[...], fl_w[...]), 0.0)
    pull = live * (RATE * jnp.concatenate([jnp.where(inside, fx[...], 0.0), sides], axis=1))
    eta = jnp.concatenate([eta2[0], eta2[1]], axis=1)
    for step in range(SUBS):
        across = [pltpu.roll(eta, 1, 1), eta, pltpu.roll(eta, 255, 1)]
        total = pull
        for q in range(3):
            turned = [pltpu.roll(across[q], 1, 0), across[q], pltpu.roll(across[q], tall - 1, 0)]
            for p in range(3):
                total = total + nrm[3 * p + q] * turned[p]
        eta = total
    eta_out[...] = eta[width:width + rows, 0:128]

    for r in order[:1] + order[:0:-1]:
        arrive(blocks[r])
        contract(partner(r)[1], False)
    if tail:
        for chunk in range(xt.shape[0]):
            for m in range(m_dev):
                h, l = split(xt[chunk, m * half:(m + 1) * half, :])
                group = pl.ds(chunk * per, per)
                high = th[m, group].reshape(128, th.shape[-1])
                low = tl[m, group].reshape(128, tl.shape[-1])
                acc[m] += dot(h, high) + dot(h, low) + dot(l, high)
    for m in range(m_dev):
        for v in range(vars_n):
            for r in range(2):
                out[m, v, :, r, :] = acc[m, pl.ds((r * vars_n + v) * lev, lev), :]
    for copy, go in remotes:
        if go is None:
            copy.wait_send()
        else:
            pl.when(go)(copy.wait_send)


def finish(spec_in, eta_in, spec_out, eta_out, sem):
    first = pltpu.make_async_copy(spec_in, spec_out, sem.at[0])
    second = pltpu.make_async_copy(eta_in, eta_out, sem.at[1])
    first.start()
    second.start()
    first.wait()
    second.wait()


def body(fourier, legendre, eta_start, coefs, wet, src_index, regrid_weight):
    n = lax.axis_size("dom")
    subs_n = lax.axis_size("sub")
    rows_n = lax.axis_size("group") * subs_n
    la, vars_n, lev, cols = fourier.shape
    m_dev, lat, ndeg = legendre.shape
    rows, blk = eta_start.shape
    pairs = vars_n * lev
    main = la // 128 * 128
    tail = la - main
    slot = -(-tail // 16) * 16 if tail else 128
    while 128 % slot:
        slot += 16
    if tail:
        assert slot * vars_n <= 128 and n % (128 // slot) == 0
    chunks = max(1, n // (128 // slot))
    count = la * cols // blk
    pad = -(-count // 8) * 8
    given = int(blk % cols != 0 or la % (blk // cols) != 0)
    more = []
    if given:
        flux = fourier[:, 0, 0, :].reshape(count, blk)
        more = [jnp.pad(flux, ((0, pad - count), (0, 0)))]
    x = jnp.transpose(fourier, (1, 2, 3, 0)).reshape(pairs * cols, la)
    index = jnp.transpose(src_index.reshape(rows, 2), (1, 0))
    weight = regrid_weight.reshape(rows, 2, blk, blk)
    depth = main // 128 * 2 * m_dev * pairs + (2 * m_dev * lev if tail else 0)
    tall = rows + 2 * SUBS
    dims = (n, rows_n, subs_n, la, pairs, cols, lev, m_dev, rows, count, slot, given)
    sends = (n - 1) * 2 + 12 + 8
    any_ = pl.BlockSpec(memory_space=pltpu.HBM)
    vmem = pl.BlockSpec(memory_space=pltpu.VMEM)
    held = [
        pltpu.with_memory_space_constraint(a, pltpu.HBM)
        for a in (x, legendre, eta_start, coefs, wet, index, weight, *more)
    ]
    spec, eta = pl.pallas_call(
        functools.partial(kernel, dims),
        out_shape=(
            jax.ShapeDtypeStruct((m_dev, vars_n, lev, 2, ndeg), F32),
            jax.ShapeDtypeStruct((rows, blk), F32),
        ),
        in_specs=[any_] * (7 + given),
        out_specs=(vmem, vmem),
        scratch_shapes=[
            pltpu.SMEM((2, rows), jnp.int32),
            pltpu.VMEM((m_dev, 2 * pairs, ndeg), F32),
            pltpu.VMEM((-(-la // 128) * 128, 128), F32),
            pltpu.VMEM((-(-la // 128), pairs * cols, 128), F32),
            pltpu.VMEM((pairs * cols, max(tail, 8)), F32),
            pltpu.VMEM(legendre.shape, F32),
            pltpu.VMEM(weight.shape, F32),
            pltpu.VMEM((n * pad, blk), F32),
            pltpu.VMEM((n - 1, depth, 128), F32),
            pltpu.VMEM((n, depth, 128), F32),
            pltpu.VMEM((m_dev, n, max(main, 16), ndeg), BF16),
            pltpu.VMEM((m_dev, n, max(main, 16), ndeg), BF16),
            pltpu.VMEM((m_dev, n, slot, ndeg), BF16),
            pltpu.VMEM((m_dev, n, slot, ndeg), BF16),
            pltpu.VMEM((chunks, 2 * m_dev * pairs, 128), F32),
            pltpu.VMEM((9, tall, blk), F32),
            pltpu.VMEM((tall, blk), jnp.int32),
            pltpu.VMEM((tall, blk), F32),
            pltpu.VMEM((tall, blk), F32),
            pltpu.VMEM((tall, blk), F32),
            pltpu.VMEM((tall, blk), F32),
            pltpu.VMEM((rows, blk), F32),
            pltpu.VMEM((rows, blk), F32),
            pltpu.VMEM((tall, blk), F32),
            pltpu.VMEM((tall, blk), F32),
            pltpu.VMEM((9, tall, 2 * blk), F32),
            pltpu.SemaphoreType.DMA((9 + main // 128 + m_dev,)),
            pltpu.SemaphoreType.DMA((sends,)),
            pltpu.SemaphoreType.DMA((sends,)),
        ],
        compiler_params=pltpu.CompilerParams(
            collective_id=0, has_side_effects=True, vmem_limit_bytes=32 * 1024 * 1024
        ),
    )(*held)
    spec, eta = pl.pallas_call(
        finish,
        out_shape=(
            jax.ShapeDtypeStruct(spec.shape, F32),
            jax.ShapeDtypeStruct(eta.shape, F32),
        ),
        in_specs=[vmem, vmem],
        out_specs=(any_, any_),
        scratch_shapes=[pltpu.SemaphoreType.DMA((2,))],
        compiler_params=pltpu.CompilerParams(vmem_limit_bytes=2 * 1024 * 1024),
    )(spec, eta)
    return spec, eta


def solution(mesh):
    placed = (
        P("dom", None, ("group", "sub"), None),
        P("dom", None, None),
        P(("group", "sub"), "dom"),
        P(None, ("group", "sub"), "dom"),
        P(("group", "sub"), "dom"),
        P(("group", "sub"), "dom", None),
        P(("group", "sub"), "dom", None, None, None),
    )
    return jax.shard_map(
        body,
        mesh=mesh,
        in_specs=placed,
        out_specs=(P("dom", None, ("group", "sub"), None, None), P(("group", "sub"), "dom")),
        check_vma=False,
    )
```

```python
import functools

import jax
import jax.numpy as jnp
from jax import lax
from jax.experimental import pallas as pl
from jax.experimental.pallas import tpu as pltpu
from jax.sharding import PartitionSpec as P

SUBS = 8
RATE = 0.5
MESH = pl.DeviceIdType.MESH
F32 = jnp.float32
BF16 = jnp.bfloat16


def split(x):
    high = x.astype(BF16)
    return high, (x - high.astype(F32)).astype(BF16)


def dot(a, b):
    return jnp.dot(a, b, preferred_element_type=F32)


def kernel(
    dims,
    *refs,
):
    x_hbm, l_hbm, eta_hbm, coef_hbm, wet_hbm, idx_hbm, w_hbm = refs[:7]
    fl_hbm = refs[7] if dims[-1] else None
    (
    out, eta_out,
    idx, acc, tr, xv, xr, lv, wv, flb, sb, rb, lh, ll, th, tl, xt, cx, wx, ex, fx, fl_w, fl_e, pk_w, pk_e, h_w, h_e, nrm,
    lsem, ssem, rsem,
    ) = refs[7 + dims[-1]:]
    n, rows_n, subs_n, la, pairs, cols, lev, m_dev, rows, count, slot, given = dims
    width = SUBS
    main = la // 128 * 128
    tail = la - main
    tiles = main // 128
    cdev = 2 * m_dev
    pad = flb.shape[0] // n
    me = lax.axis_index("dom")
    row = lax.axis_index("group") * subs_n + lax.axis_index("sub")

    def at(drow, ddom):
        target = {}
        if drow:
            other = lax.rem(row + rows_n + drow, rows_n)
            target["group"] = other // subs_n
            target["sub"] = lax.rem(other, subs_n)
        if ddom:
            target["dom"] = lax.rem(me + n + ddom, n)
        return target

    locals_ = []

    def fetch(src, dst):
        copy = pltpu.make_async_copy(src, dst, lsem.at[len(locals_)])
        locals_.append(copy)
        copy.start()
        return copy

    remotes = []

    def send(src, dst, target, ddom=0):
        i = len(remotes)
        copy = pltpu.make_async_remote_copy(
            src_ref=src, dst_ref=dst, send_sem=ssem.at[i], recv_sem=rsem.at[i],
            device_id=target, device_id_type=MESH,
        )
        go = {1: me < n - 1, -1: me > 0}.get(ddom)
        come = {1: me > 0, -1: me < n - 1}.get(ddom)
        remotes.append((copy, go))
        if go is None:
            copy.start()
        else:
            pl.when(go)(copy.start)
        return copy, come

    def arrive(sent):
        copy, come = sent
        if come is None:
            copy.wait_recv()
        else:
            pl.when(come)(copy.wait_recv)

    def partner(r):
        if n & (n - 1):
            return lax.rem(me + r, n), lax.rem(me + n - r, n)
        other = me
        bit = 1
        while bit < n:
            if r & bit:
                other = other + bit - 2 * bit * lax.rem(me // bit, 2)
            bit *= 2
        return other, other

    barrier = pltpu.get_barrier_semaphore()
    greet = [at(0, r) for r in range(1, n)]
    greet += [at(dr, dd) for dr in (-1, 1) for dd in (-1, 0, 1)]
    for target in greet:
        pl.semaphore_signal(barrier, inc=1, device_id=target, device_id_type=MESH)
    get_c = fetch(coef_hbm, cx.at[:, pl.ds(width, rows), :])
    get_w = fetch(wet_hbm, wx.at[pl.ds(width, rows), :])
    get_e = fetch(eta_hbm, ex.at[pl.ds(width, rows), :])
    get_x = [fetch(x_hbm.at[:, pl.ds(t * 128, 128)], xv.at[t]) for t in range(tiles)]
    if tail:
        get_x.append(fetch(x_hbm.at[:, pl.ds(main, tail)], xr))
    mine = pl.ds(pl.multiple_of(me * pad, 8), pad)
    get_f = fetch(fl_hbm, flb.at[mine, :]) if given else None
    get_r = [fetch(idx_hbm, idx), fetch(w_hbm, wv)]
    get_l = [fetch(l_hbm.at[m], lv.at[m]) for m in range(m_dev)]

    lane = lax.broadcasted_iota(jnp.int32, (1, 128), 1)
    get_c.wait()
    get_w.wait()
    get_e.wait()
    own = pl.ds(width, rows)
    planes = [cx[k, own, :] for k in range(9)] + [wx[own, :].astype(F32), ex[own, :]]
    left = jnp.zeros((rows, 128), F32)
    right = jnp.zeros((rows, 128), F32)
    for p, plane in enumerate(planes):
        here = (lane >= width * p) & (lane < width * (p + 1))
        left = jnp.where(here, pltpu.roll(plane, width * p, 1), left)
        right = jnp.where(here, pltpu.roll(plane, (width * p + width) % 128, 1), right)
    pk_w[...] = left
    pk_e[...] = right

    for copy in get_x:
        copy.wait()
    vars_n = pairs // lev
    if tail:
        xv[tiles] = jnp.concatenate([xr[...], jnp.zeros((xr.shape[0], 128 - tail), F32)], axis=1)
    if given:
        get_f.wait()
    else:
        group = 128 // cols
        for t in range(xv.shape[0]):
            plane = jnp.concatenate([xv[t, 0:cols, :], jnp.zeros((128 - cols, 128), F32)], axis=0)
            tr[t * 128:(t + 1) * 128, :] = plane.T
        flux = tr[pl.ds(0, pad, stride=group), :]
        for g in range(1, group):
            flux = flux + pltpu.roll(tr[pl.ds(g, pad, stride=group), :], cols * g, 1)
        flb[mine, :] = flux

    def pack(dest, store):
        for c in range(cdev):
            where = dest * cdev + c
            for t in range(tiles):
                store(
                    t * cdev * pairs + c * pairs, pairs,
                    xv.at[t][pl.ds(where, pairs, stride=cols), :],
                )
            if tail:
                rest = xv.at[tiles][pl.ds(where, pairs, stride=cols), :]
                total = rest[0:lev]
                for v in range(1, vars_n):
                    total = total + pltpu.roll(rest[v * lev:(v + 1) * lev], slot * v, 1)
                store(tiles * cdev * pairs + c * lev, lev, total)

    def keep(buffer, which):
        def store(first, height, value):
            buffer[which, pl.ds(first, height), :] = value
        return store

    order = sorted(range(1, n), key=lambda r: (r < n // 2, r))
    for r in order:
        pack(partner(r)[0], keep(sb, r - 1))
    pack(me, keep(rb, me))
    blocks = {r: [] for r in order}
    depth = sb.shape[1]
    cut = depth // 16 * 8
    head, rear = pl.ds(0, cut), pl.ds(cut, depth - cut)

    def send_block(r, *parts):
        for part in parts:
            blocks[r].append(
                send(sb.at[r - 1, part, :], rb.at[me, part, :], at_dom(partner(r)[0]))
            )

    def at_dom(other):
        return {"dom": other}

    pl.semaphore_wait(barrier, len(greet))
    top, bottom = pl.ds(0, width), pl.ds(rows - width, width)
    halo_n, halo_s = pl.ds(0, width), pl.ds(width + rows, width)
    relay = n == 4
    get_flux = [
        send(flb.at[mine, :], flb.at[mine, :], at_dom(partner(r)[0]))
        for r in order if r < 3 or not relay
    ]
    edges = []
    for src, dst in ((coef_hbm, cx), ):
        edges.append(send(src.at[:, bottom, :], dst.at[:, halo_n, :], at(1, 0)))
        edges.append(send(src.at[:, top, :], dst.at[:, halo_s, :], at(-1, 0)))
    for src, dst in ((wet_hbm, wx), (eta_hbm, ex)):
        edges.append(send(src.at[bottom, :], dst.at[halo_n, :], at(1, 0)))
        edges.append(send(src.at[top, :], dst.at[halo_s, :], at(-1, 0)))
    for src, dst, dd in ((pk_e, h_w, 1), (pk_w, h_e, -1)):
        edges.append(send(src, dst.at[own, :], at(0, dd), dd))
        edges.append(send(src.at[bottom, :], dst.at[halo_n, :], at(1, dd), dd))
        edges.append(send(src.at[top, :], dst.at[halo_s, :], at(-1, dd), dd))

    send_block(order[0], head, rear)
    send_block(order[1], head)

    for copy in get_l:
        copy.wait()
    per = 128 // slot

    def split_legendre(d, carry):
        for m in range(m_dev):
            if main:
                h, l = split(lv[m, pl.ds(pl.multiple_of(d * la, 8), main), :])
                lh[m, d] = h
                ll[m, d] = l
            if tail:
                part = lv[m, pl.ds(pl.multiple_of(d * la + main, 8), tail), :]
                if slot > tail:
                    part = jnp.concatenate([part, jnp.zeros((slot - tail, part.shape[1]), F32)], axis=0)
                h, l = split(part)
                th[m, d] = h
                tl[m, d] = l
        return carry

    lax.fori_loop(0, n // 2, split_legendre, 0)
    if relay:
        arrive(get_flux[0])
        across = pl.ds(pl.multiple_of(partner(2)[0] * pad, 8), pad)
        get_flux = get_flux[1:] + [send(flb.at[across, :], flb.at[across, :], at_dom(partner(1)[0]))]
    lax.fori_loop(n // 2, n, split_legendre, 0)

    for copy in get_flux:
        arrive(copy)
    for copy in get_r:
        copy.wait()

    def regrid(i, total):
        part = None
        for k in range(2):
            block = idx[k, i]
            at_row = (block // count) * pad + lax.rem(block, count)
            term = wv[i, k] * flb[pl.ds(at_row, 1), :]
            part = term if part is None else part + term
        return jnp.where(lane == i, jnp.sum(part, axis=1, keepdims=True), total)

    forced = lax.fori_loop(0, rows, regrid, jnp.zeros((128, 128), F32))
    fx[own, :] = forced.T[0:rows]
    up, down = pl.ds(width, width), pl.ds(rows, width)
    force = []
    force.append(send(fx.at[down, :], fx.at[halo_n, :], at(1, 0)))
    force.append(send(fx.at[up, :], fx.at[halo_s, :], at(-1, 0)))
    for dst, dd in ((fl_w, 1), (fl_e, -1)):
        force.append(send(fx.at[own, :], dst.at[own, :], at(0, dd), dd))
        force.append(send(fx.at[down, :], dst.at[halo_n, :], at(1, dd), dd))
        force.append(send(fx.at[up, :], dst.at[halo_s, :], at(-1, dd), dd))

    send_block(order[1], rear)
    for r in order[2:]:
        send_block(r, head, rear)

    for copy in edges:
        arrive(copy)
    tall = rows + 2 * width
    spot = lax.broadcasted_iota(jnp.int32, (tall, 128), 0) + row * rows - width
    lanes = lax.broadcasted_iota(jnp.int32, (tall, 128), 1)
    inside = (spot >= 0) & (spot < rows_n * rows)
    is_e = lanes < width
    is_w = lanes >= 128 - width
    side_in = inside & ((is_e & (me < n - 1)) | (is_w & (me > 0)))
    west, east = h_w[...], h_e[...]

    def side(p):
        from_e = pltpu.roll(east, (128 - width * p) % 128, 1)
        from_w = pltpu.roll(west, (256 - width - width * p) % 128, 1)
        return jnp.where(is_e, from_e, from_w)

    def extend(middle, p, other):
        return (
            jnp.where(inside, middle, other),
            jnp.where(side_in, side(p), other),
        )

    coefs = [extend(cx[k], k, 1.0) for k in range(9)]
    mask = extend(wx[...].astype(F32), 9, 0.0)
    eta2 = extend(ex[...], 10, 0.0)
    for h in range(2):
        scale = mask[h] / functools.reduce(lambda a, b: a + b, [c[h] for c in coefs])
        for k in range(9):
            nrm[k, :, h * 128:(h + 1) * 128] = coefs[k][h] * scale

    half = 2 * pairs

    def contract(d, first):
        for m in range(m_dev):
            if main:
                parts = [
                    rb[d, pl.ds(t * cdev * pairs + m * half, half), :] for t in range(tiles)
                ]
                h, l = split(jnp.concatenate(parts, axis=1) if tiles > 1 else parts[0])
                value = dot(h, lh[m, d]) + dot(h, ll[m, d]) + dot(l, lh[m, d])
                if first:
                    acc[m] = value
                else:
                    acc[m] += value
            elif first:
                acc[m] = jnp.zeros_like(acc[m])
        if tail:
            e = lax.rem(d, per)
            chunk = d // per
            for c in range(cdev):
                packed = rb[d, pl.ds(tiles * cdev * pairs + c * lev, lev), :]
                for v in range(vars_n):
                    turn = lax.rem((e - v) * slot + 128 * vars_n, 128)
                    moved = pltpu.roll(packed, turn, 1)
                    place = pl.ds(c * pairs + v * lev, lev)
                    here = (lane >= e * slot) & (lane < (e + 1) * slot)
                    xt[chunk, place, :] = jnp.where(here, moved, xt[chunk, place, :])

    if tail:
        xt[...] = jnp.zeros_like(xt)
    contract(me, True)

    def receive(r):
        for part in blocks[r]:
            arrive(part)
        contract(partner(r)[1], False)

    receive(order[0])

    for copy in force:
        arrive(copy)
    live = jnp.concatenate([mask[0], mask[1]], axis=1)
    sides = jnp.where(side_in, jnp.where(is_e, fl_e[...], fl_w[...]), 0.0)
    pull = live * (RATE * jnp.concatenate([jnp.where(inside, fx[...], 0.0), sides], axis=1))
    eta = jnp.concatenate([eta2[0], eta2[1]], axis=1)
    for step in range(SUBS):
        across = [pltpu.roll(eta, 1, 1), eta, pltpu.roll(eta, 255, 1)]
        total = pull
        for q in range(3):
            turned = [pltpu.roll(across[q], 1, 0), across[q], pltpu.roll(across[q], tall - 1, 0)]
            for p in range(3):
                total = total + nrm[3 * p + q] * turned[p]
        eta = total
    eta_out[...] = eta[width:width + rows, 0:128]

    for r in order[:0:-1]:
        receive(r)
    if tail:
        for chunk in range(xt.shape[0]):
            for m in range(m_dev):
                h, l = split(xt[chunk, m * half:(m + 1) * half, :])
                group = pl.ds(chunk * per, per)
                high = th[m, group].reshape(128, th.shape[-1])
                low = tl[m, group].reshape(128, tl.shape[-1])
                acc[m] += dot(h, high) + dot(h, low) + dot(l, high)
    for m in range(m_dev):
        for v in range(vars_n):
            for r in range(2):
                out[m, v, :, r, :] = acc[m, pl.ds((r * vars_n + v) * lev, lev), :]
    for copy, go in remotes:
        if go is None:
            copy.wait_send()
        else:
            pl.when(go)(copy.wait_send)


def finish(spec_in, eta_in, spec_out, eta_out, sem):
    first = pltpu.make_async_copy(spec_in, spec_out, sem.at[0])
    second = pltpu.make_async_copy(eta_in, eta_out, sem.at[1])
    first.start()
    second.start()
    first.wait()
    second.wait()


def body(fourier, legendre, eta_start, coefs, wet, src_index, regrid_weight):
    n = lax.axis_size("dom")
    subs_n = lax.axis_size("sub")
    rows_n = lax.axis_size("group") * subs_n
    la, vars_n, lev, cols = fourier.shape
    m_dev, lat, ndeg = legendre.shape
    rows, blk = eta_start.shape
    pairs = vars_n * lev
    main = la // 128 * 128
    tail = la - main
    slot = -(-tail // 16) * 16 if tail else 128
    while 128 % slot:
        slot += 16
    if tail:
        assert slot * vars_n <= 128 and n % (128 // slot) == 0
    chunks = max(1, n // (128 // slot))
    count = la * cols // blk
    pad = -(-count // 8) * 8
    given = int(blk % cols != 0 or la % (blk // cols) != 0)
    more = []
    if given:
        flux = fourier[:, 0, 0, :].reshape(count, blk)
        more = [jnp.pad(flux, ((0, pad - count), (0, 0)))]
    x = jnp.transpose(fourier, (1, 2, 3, 0)).reshape(pairs * cols, la)
    index = jnp.transpose(src_index.reshape(rows, 2), (1, 0))
    weight = regrid_weight.reshape(rows, 2, blk, blk)
    depth = main // 128 * 2 * m_dev * pairs + (2 * m_dev * lev if tail else 0)
    tall = rows + 2 * SUBS
    dims = (n, rows_n, subs_n, la, pairs, cols, lev, m_dev, rows, count, slot, given)
    sends = (n - 1) * 3 + 12 + 8
    any_ = pl.BlockSpec(memory_space=pltpu.HBM)
    vmem = pl.BlockSpec(memory_space=pltpu.VMEM)
    held = [
        pltpu.with_memory_space_constraint(a, pltpu.HBM)
        for a in (x, legendre, eta_start, coefs, wet, index, weight, *more)
    ]
    spec, eta = pl.pallas_call(
        functools.partial(kernel, dims),
        out_shape=(
            jax.ShapeDtypeStruct((m_dev, vars_n, lev, 2, ndeg), F32),
            jax.ShapeDtypeStruct((rows, blk), F32),
        ),
        in_specs=[any_] * (7 + given),
        out_specs=(vmem, vmem),
        scratch_shapes=[
            pltpu.SMEM((2, rows), jnp.int32),
            pltpu.VMEM((m_dev, 2 * pairs, ndeg), F32),
            pltpu.VMEM((-(-la // 128) * 128, 128), F32),
            pltpu.VMEM((-(-la // 128), pairs * cols, 128), F32),
            pltpu.VMEM((pairs * cols, max(tail, 8)), F32),
            pltpu.VMEM(legendre.shape, F32),
            pltpu.VMEM(weight.shape, F32),
            pltpu.VMEM((n * pad, blk), F32),
            pltpu.VMEM((n - 1, depth, 128), F32),
            pltpu.VMEM((n, depth, 128), F32),
            pltpu.VMEM((m_dev, n, max(main, 16), ndeg), BF16),
            pltpu.VMEM((m_dev, n, max(main, 16), ndeg), BF16),
            pltpu.VMEM((m_dev, n, slot, ndeg), BF16),
            pltpu.VMEM((m_dev, n, slot, ndeg), BF16),
            pltpu.VMEM((chunks, 2 * m_dev * pairs, 128), F32),
            pltpu.VMEM((9, tall, blk), F32),
            pltpu.VMEM((tall, blk), jnp.int32),
            pltpu.VMEM((tall, blk), F32),
            pltpu.VMEM((tall, blk), F32),
            pltpu.VMEM((tall, blk), F32),
            pltpu.VMEM((tall, blk), F32),
            pltpu.VMEM((rows, blk), F32),
            pltpu.VMEM((rows, blk), F32),
            pltpu.VMEM((tall, blk), F32),
            pltpu.VMEM((tall, blk), F32),
            pltpu.VMEM((9, tall, 2 * blk), F32),
            pltpu.SemaphoreType.DMA((9 + main // 128 + m_dev,)),
            pltpu.SemaphoreType.DMA((sends,)),
            pltpu.SemaphoreType.DMA((sends,)),
        ],
        compiler_params=pltpu.CompilerParams(
            collective_id=0, has_side_effects=True, vmem_limit_bytes=32 * 1024 * 1024
        ),
    )(*held)
    spec, eta = pl.pallas_call(
        finish,
        out_shape=(
            jax.ShapeDtypeStruct(spec.shape, F32),
            jax.ShapeDtypeStruct(eta.shape, F32),
        ),
        in_specs=[vmem, vmem],
        out_specs=(any_, any_),
        scratch_shapes=[pltpu.SemaphoreType.DMA((2,))],
        compiler_params=pltpu.CompilerParams(vmem_limit_bytes=2 * 1024 * 1024),
    )(spec, eta)
    return spec, eta


def solution(mesh):
    placed = (
        P("dom", None, ("group", "sub"), None),
        P("dom", None, None),
        P(("group", "sub"), "dom"),
        P(None, ("group", "sub"), "dom"),
        P(("group", "sub"), "dom"),
        P(("group", "sub"), "dom", None),
        P(("group", "sub"), "dom", None, None, None),
    )
    return jax.shard_map(
        body,
        mesh=mesh,
        in_specs=placed,
        out_specs=(P("dom", None, ("group", "sub"), None, None), P(("group", "sub"), "dom")),
        check_vma=False,
    )
```

```python
import functools

import jax
import jax.numpy as jnp
from jax import lax
from jax.experimental import pallas as pl
from jax.experimental.pallas import tpu as pltpu
from jax.sharding import PartitionSpec as P

SUBS = 8
RATE = 0.5
MESH = pl.DeviceIdType.MESH
F32 = jnp.float32
BF16 = jnp.bfloat16


def split(x):
    high = x.astype(BF16)
    return high, (x - high.astype(F32)).astype(BF16)


def dot(a, b):
    return jnp.dot(a, b, preferred_element_type=F32)


def kernel(
    dims,
    *refs,
):
    x_hbm, l_hbm, eta_hbm, coef_hbm, wet_hbm, idx_hbm, w_hbm = refs[:7]
    fl_hbm = refs[7] if dims[-1] else None
    (
    out, eta_out,
    idx, acc, tr, xv, xr, lv, wv, flb, sb, rb, lh, ll, th, tl, xt, cx, wx, ex, fx, fl_w, fl_e, pk_w, pk_e, h_w, h_e, nrm,
    lsem, ssem, rsem,
    ) = refs[7 + dims[-1]:]
    n, rows_n, subs_n, la, pairs, cols, lev, m_dev, rows, count, slot, given = dims
    width = SUBS
    main = la // 128 * 128
    tail = la - main
    tiles = main // 128
    cdev = 2 * m_dev
    pad = flb.shape[0] // n
    me = lax.axis_index("dom")
    row = lax.axis_index("group") * subs_n + lax.axis_index("sub")

    def at(drow, ddom):
        target = {}
        if drow:
            other = lax.rem(row + rows_n + drow, rows_n)
            target["group"] = other // subs_n
            target["sub"] = lax.rem(other, subs_n)
        if ddom:
            target["dom"] = lax.rem(me + n + ddom, n)
        return target

    locals_ = []

    def fetch(src, dst):
        copy = pltpu.make_async_copy(src, dst, lsem.at[len(locals_)])
        locals_.append(copy)
        copy.start()
        return copy

    remotes = []

    def send(src, dst, target, ddom=0):
        i = len(remotes)
        copy = pltpu.make_async_remote_copy(
            src_ref=src, dst_ref=dst, send_sem=ssem.at[i], recv_sem=rsem.at[i],
            device_id=target, device_id_type=MESH,
        )
        go = {1: me < n - 1, -1: me > 0}.get(ddom)
        come = {1: me > 0, -1: me < n - 1}.get(ddom)
        remotes.append((copy, go))
        if go is None:
            copy.start()
        else:
            pl.when(go)(copy.start)
        return copy, come

    def arrive(sent):
        copy, come = sent
        if come is None:
            copy.wait_recv()
        else:
            pl.when(come)(copy.wait_recv)

    def partner(r):
        if n & (n - 1):
            return lax.rem(me + r, n), lax.rem(me + n - r, n)
        other = me
        bit = 1
        while bit < n:
            if r & bit:
                other = other + bit - 2 * bit * lax.rem(me // bit, 2)
            bit *= 2
        return other, other

    get_x = [fetch(x_hbm.at[:, pl.ds(t * 128, 128)], xv.at[t]) for t in range(tiles)]
    if tail:
        get_x.append(fetch(x_hbm.at[:, pl.ds(main, tail)], xr))
    barrier = pltpu.get_barrier_semaphore()
    greet = [at(0, r) for r in range(1, n)]
    greet += [at(dr, dd) for dr in (-1, 1) for dd in (-1, 0, 1)]
    for target in greet:
        pl.semaphore_signal(barrier, inc=1, device_id=target, device_id_type=MESH)
    get_c = fetch(coef_hbm, cx.at[:, pl.ds(width, rows), :])
    get_w = fetch(wet_hbm, wx.at[pl.ds(width, rows), :])
    get_e = fetch(eta_hbm, ex.at[pl.ds(width, rows), :])
    mine = pl.ds(pl.multiple_of(me * pad, 8), pad)
    get_f = fetch(fl_hbm, flb.at[mine, :]) if given else None

    lane = lax.broadcasted_iota(jnp.int32, (1, 128), 1)
    get_c.wait()
    get_w.wait()
    get_e.wait()
    own = pl.ds(width, rows)
    planes = [cx[k, own, :] for k in range(9)] + [wx[own, :].astype(F32), ex[own, :]]
    left = jnp.zeros((rows, 128), F32)
    right = jnp.zeros((rows, 128), F32)
    for p, plane in enumerate(planes):
        here = (lane >= width * p) & (lane < width * (p + 1))
        left = jnp.where(here, pltpu.roll(plane, width * p, 1), left)
        right = jnp.where(here, pltpu.roll(plane, (width * p + width) % 128, 1), right)
    pk_w[...] = left
    pk_e[...] = right

    for copy in get_x:
        copy.wait()
    get_r = [fetch(idx_hbm, idx), fetch(w_hbm, wv)]
    get_l = [fetch(l_hbm.at[m], lv.at[m]) for m in range(m_dev)]
    vars_n = pairs // lev
    if tail:
        xv[tiles] = jnp.concatenate([xr[...], jnp.zeros((xr.shape[0], 128 - tail), F32)], axis=1)
    if given:
        get_f.wait()
    else:
        group = 128 // cols
        for t in range(xv.shape[0]):
            plane = jnp.concatenate([xv[t, 0:cols, :], jnp.zeros((128 - cols, 128), F32)], axis=0)
            tr[t * 128:(t + 1) * 128, :] = plane.T
        flux = tr[pl.ds(0, pad, stride=group), :]
        for g in range(1, group):
            flux = flux + pltpu.roll(tr[pl.ds(g, pad, stride=group), :], cols * g, 1)
        flb[mine, :] = flux

    def pack(dest, store):
        for c in range(cdev):
            where = dest * cdev + c
            for t in range(tiles):
                store(
                    t * cdev * pairs + c * pairs, pairs,
                    xv.at[t][pl.ds(where, pairs, stride=cols), :],
                )
            if tail:
                rest = xv.at[tiles][pl.ds(where, pairs, stride=cols), :]
                total = rest[0:lev]
                for v in range(1, vars_n):
                    total = total + pltpu.roll(rest[v * lev:(v + 1) * lev], slot * v, 1)
                store(tiles * cdev * pairs + c * lev, lev, total)

    def keep(buffer, which):
        def store(first, height, value):
            buffer[which, pl.ds(first, height), :] = value
        return store

    order = sorted(range(1, n), key=lambda r: (r < n // 2, r))
    pack(partner(order[0])[0], keep(sb, order[0] - 1))
    blocks = {r: [] for r in order}
    depth = sb.shape[1]
    cut = depth // 16 * 8
    head, rear = pl.ds(0, cut), pl.ds(cut, depth - cut)

    def send_block(r, *parts):
        for part in parts:
            blocks[r].append(
                send(sb.at[r - 1, part, :], rb.at[me, part, :], at_dom(partner(r)[0]))
            )

    def at_dom(other):
        return {"dom": other}

    pl.semaphore_wait(barrier, len(greet))
    top, bottom = pl.ds(0, width), pl.ds(rows - width, width)
    halo_n, halo_s = pl.ds(0, width), pl.ds(width + rows, width)
    get_flux = [
        send(flb.at[mine, :], flb.at[mine, :], at_dom(partner(r)[0]))
        for r in order
    ]
    edges = []
    for src, dst in ((coef_hbm, cx), ):
        edges.append(send(src.at[:, bottom, :], dst.at[:, halo_n, :], at(1, 0)))
        edges.append(send(src.at[:, top, :], dst.at[:, halo_s, :], at(-1, 0)))
    for src, dst in ((wet_hbm, wx), (eta_hbm, ex)):
        edges.append(send(src.at[bottom, :], dst.at[halo_n, :], at(1, 0)))
        edges.append(send(src.at[top, :], dst.at[halo_s, :], at(-1, 0)))
    for src, dst, dd in ((pk_e, h_w, 1), (pk_w, h_e, -1)):
        edges.append(send(src, dst.at[own, :], at(0, dd), dd))
        edges.append(send(src.at[bottom, :], dst.at[halo_n, :], at(1, dd), dd))
        edges.append(send(src.at[top, :], dst.at[halo_s, :], at(-1, dd), dd))

    send_block(order[0], head, rear)
    for r in order[1:]:
        pack(partner(r)[0], keep(sb, r - 1))
    send_block(order[1], head)
    pack(me, keep(rb, me))

    for copy in get_l:
        copy.wait()
    per = 128 // slot

    def split_legendre(d, carry):
        for m in range(m_dev):
            if main:
                h, l = split(lv[m, pl.ds(pl.multiple_of(d * la, 8), main), :])
                lh[m, d] = h
                ll[m, d] = l
            if tail:
                part = lv[m, pl.ds(pl.multiple_of(d * la + main, 8), tail), :]
                if slot > tail:
                    part = jnp.concatenate([part, jnp.zeros((slot - tail, part.shape[1]), F32)], axis=0)
                h, l = split(part)
                th[m, d] = h
                tl[m, d] = l
        return carry

    lax.fori_loop(0, n, split_legendre, 0)

    for copy in get_flux:
        arrive(copy)
    for copy in get_r:
        copy.wait()

    def regrid(i, total):
        part = None
        for k in range(2):
            block = idx[k, i]
            at_row = (block // count) * pad + lax.rem(block, count)
            term = wv[i, k] * flb[pl.ds(at_row, 1), :]
            part = term if part is None else part + term
        return jnp.where(lane == i, jnp.sum(part, axis=1, keepdims=True), total)

    forced = lax.fori_loop(0, rows, regrid, jnp.zeros((128, 128), F32), unroll=4)
    fx[own, :] = forced.T[0:rows]
    up, down = pl.ds(width, width), pl.ds(rows, width)
    force = []
    force.append(send(fx.at[down, :], fx.at[halo_n, :], at(1, 0)))
    force.append(send(fx.at[up, :], fx.at[halo_s, :], at(-1, 0)))
    for dst, dd in ((fl_w, 1), (fl_e, -1)):
        force.append(send(fx.at[own, :], dst.at[own, :], at(0, dd), dd))
        force.append(send(fx.at[down, :], dst.at[halo_n, :], at(1, dd), dd))
        force.append(send(fx.at[up, :], dst.at[halo_s, :], at(-1, dd), dd))

    send_block(order[1], rear)
    for r in order[2:]:
        send_block(r, head, rear)

    for copy in edges:
        arrive(copy)
    tall = rows + 2 * width
    spot = lax.broadcasted_iota(jnp.int32, (tall, 128), 0) + row * rows - width
    lanes = lax.broadcasted_iota(jnp.int32, (tall, 128), 1)
    inside = (spot >= 0) & (spot < rows_n * rows)
    is_e = lanes < width
    is_w = lanes >= 128 - width
    side_in = inside & ((is_e & (me < n - 1)) | (is_w & (me > 0)))
    west, east = h_w[...], h_e[...]

    def side(p):
        from_e = pltpu.roll(east, (128 - width * p) % 128, 1)
        from_w = pltpu.roll(west, (256 - width - width * p) % 128, 1)
        return jnp.where(is_e, from_e, from_w)

    def extend(middle, p, other):
        return (
            jnp.where(inside, middle, other),
            jnp.where(side_in, side(p), other),
        )

    coefs = [extend(cx[k], k, 1.0) for k in range(9)]
    mask = extend(wx[...].astype(F32), 9, 0.0)
    eta2 = extend(ex[...], 10, 0.0)
    for h in range(2):
        scale = mask[h] / functools.reduce(lambda a, b: a + b, [c[h] for c in coefs])
        for k in range(9):
            nrm[k, :, h * 128:(h + 1) * 128] = coefs[k][h] * scale

    half = 2 * pairs

    def contract(d, first):
        for m in range(m_dev):
            if main:
                parts = [
                    rb[d, pl.ds(t * cdev * pairs + m * half, half), :] for t in range(tiles)
                ]
                h, l = split(jnp.concatenate(parts, axis=1) if tiles > 1 else parts[0])
                value = dot(h, lh[m, d]) + dot(h, ll[m, d]) + dot(l, lh[m, d])
                if first:
                    acc[m] = value
                else:
                    acc[m] += value
            elif first:
                acc[m] = jnp.zeros_like(acc[m])
        if tail:
            e = lax.rem(d, per)
            chunk = d // per
            for c in range(cdev):
                packed = rb[d, pl.ds(tiles * cdev * pairs + c * lev, lev), :]
                for v in range(vars_n):
                    turn = lax.rem((e - v) * slot + 128 * vars_n, 128)
                    moved = pltpu.roll(packed, turn, 1)
                    place = pl.ds(c * pairs + v * lev, lev)
                    here = (lane >= e * slot) & (lane < (e + 1) * slot)
                    xt[chunk, place, :] = jnp.where(here, moved, xt[chunk, place, :])

    if tail:
        xt[...] = jnp.zeros_like(xt)
    contract(me, True)

    def receive(r):
        for part in blocks[r]:
            arrive(part)
        contract(partner(r)[1], False)

    receive(order[0])

    for copy in force:
        arrive(copy)
    live = jnp.concatenate([mask[0], mask[1]], axis=1)
    sides = jnp.where(side_in, jnp.where(is_e, fl_e[...], fl_w[...]), 0.0)
    pull = live * (RATE * jnp.concatenate([jnp.where(inside, fx[...], 0.0), sides], axis=1))
    eta = jnp.concatenate([eta2[0], eta2[1]], axis=1)
    for step in range(SUBS):
        across = [pltpu.roll(eta, 1, 1), eta, pltpu.roll(eta, 255, 1)]
        total = pull
        for q in range(3):
            turned = [pltpu.roll(across[q], 1, 0), across[q], pltpu.roll(across[q], tall - 1, 0)]
            for p in range(3):
                total = total + nrm[3 * p + q] * turned[p]
        eta = total
    eta_out[...] = eta[width:width + rows, 0:128]

    for r in order[:0:-1]:
        receive(r)
    if tail:
        for chunk in range(xt.shape[0]):
            for m in range(m_dev):
                h, l = split(xt[chunk, m * half:(m + 1) * half, :])
                group = pl.ds(chunk * per, per)
                high = th[m, group].reshape(128, th.shape[-1])
                low = tl[m, group].reshape(128, tl.shape[-1])
                acc[m] += dot(h, high) + dot(h, low) + dot(l, high)
    for m in range(m_dev):
        for v in range(vars_n):
            for r in range(2):
                out[m, v, :, r, :] = acc[m, pl.ds((r * vars_n + v) * lev, lev), :]
    for copy, go in remotes:
        if go is None:
            copy.wait_send()
        else:
            pl.when(go)(copy.wait_send)


def finish(spec_in, eta_in, spec_out, eta_out, sem):
    first = pltpu.make_async_copy(spec_in, spec_out, sem.at[0])
    second = pltpu.make_async_copy(eta_in, eta_out, sem.at[1])
    first.start()
    second.start()
    first.wait()
    second.wait()


def body(fourier, legendre, eta_start, coefs, wet, src_index, regrid_weight):
    n = lax.axis_size("dom")
    subs_n = lax.axis_size("sub")
    rows_n = lax.axis_size("group") * subs_n
    la, vars_n, lev, cols = fourier.shape
    m_dev, lat, ndeg = legendre.shape
    rows, blk = eta_start.shape
    pairs = vars_n * lev
    main = la // 128 * 128
    tail = la - main
    slot = -(-tail // 16) * 16 if tail else 128
    while 128 % slot:
        slot += 16
    if tail:
        assert slot * vars_n <= 128 and n % (128 // slot) == 0
    chunks = max(1, n // (128 // slot))
    count = la * cols // blk
    pad = -(-count // 8) * 8
    given = int(blk % cols != 0 or la % (blk // cols) != 0)
    more = []
    if given:
        flux = fourier[:, 0, 0, :].reshape(count, blk)
        more = [jnp.pad(flux, ((0, pad - count), (0, 0)))]
    x = jnp.transpose(fourier, (1, 2, 3, 0)).reshape(pairs * cols, la)
    index = jnp.transpose(src_index.reshape(rows, 2), (1, 0))
    weight = regrid_weight.reshape(rows, 2, blk, blk)
    depth = main // 128 * 2 * m_dev * pairs + (2 * m_dev * lev if tail else 0)
    tall = rows + 2 * SUBS
    dims = (n, rows_n, subs_n, la, pairs, cols, lev, m_dev, rows, count, slot, given)
    sends = (n - 1) * 3 + 12 + 8
    any_ = pl.BlockSpec(memory_space=pltpu.HBM)
    vmem = pl.BlockSpec(memory_space=pltpu.VMEM)
    held = [
        pltpu.with_memory_space_constraint(a, pltpu.HBM)
        for a in (x, legendre, eta_start, coefs, wet, index, weight, *more)
    ]
    spec, eta = pl.pallas_call(
        functools.partial(kernel, dims),
        out_shape=(
            jax.ShapeDtypeStruct((m_dev, vars_n, lev, 2, ndeg), F32),
            jax.ShapeDtypeStruct((rows, blk), F32),
        ),
        in_specs=[any_] * (7 + given),
        out_specs=(vmem, vmem),
        scratch_shapes=[
            pltpu.SMEM((2, rows), jnp.int32),
            pltpu.VMEM((m_dev, 2 * pairs, ndeg), F32),
            pltpu.VMEM((-(-la // 128) * 128, 128), F32),
            pltpu.VMEM((-(-la // 128), pairs * cols, 128), F32),
            pltpu.VMEM((pairs * cols, max(tail, 8)), F32),
            pltpu.VMEM(legendre.shape, F32),
            pltpu.VMEM(weight.shape, F32),
            pltpu.VMEM((n * pad, blk), F32),
            pltpu.VMEM((n - 1, depth, 128), F32),
            pltpu.VMEM((n, depth, 128), F32),
            pltpu.VMEM((m_dev, n, max(main, 16), ndeg), BF16),
            pltpu.VMEM((m_dev, n, max(main, 16), ndeg), BF16),
            pltpu.VMEM((m_dev, n, slot, ndeg), BF16),
            pltpu.VMEM((m_dev, n, slot, ndeg), BF16),
            pltpu.VMEM((chunks, 2 * m_dev * pairs, 128), F32),
            pltpu.VMEM((9, tall, blk), F32),
            pltpu.VMEM((tall, blk), jnp.int32),
            pltpu.VMEM((tall, blk), F32),
            pltpu.VMEM((tall, blk), F32),
            pltpu.VMEM((tall, blk), F32),
            pltpu.VMEM((tall, blk), F32),
            pltpu.VMEM((rows, blk), F32),
            pltpu.VMEM((rows, blk), F32),
            pltpu.VMEM((tall, blk), F32),
            pltpu.VMEM((tall, blk), F32),
            pltpu.VMEM((9, tall, 2 * blk), F32),
            pltpu.SemaphoreType.DMA((9 + main // 128 + m_dev,)),
            pltpu.SemaphoreType.DMA((sends,)),
            pltpu.SemaphoreType.DMA((sends,)),
        ],
        compiler_params=pltpu.CompilerParams(
            collective_id=0, has_side_effects=True, vmem_limit_bytes=32 * 1024 * 1024
        ),
    )(*held)
    spec, eta = pl.pallas_call(
        finish,
        out_shape=(
            jax.ShapeDtypeStruct(spec.shape, F32),
            jax.ShapeDtypeStruct(eta.shape, F32),
        ),
        in_specs=[vmem, vmem],
        out_specs=(any_, any_),
        scratch_shapes=[pltpu.SemaphoreType.DMA((2,))],
        compiler_params=pltpu.CompilerParams(vmem_limit_bytes=2 * 1024 * 1024),
    )(spec, eta)
    return spec, eta


def solution(mesh):
    placed = (
        P("dom", None, ("group", "sub"), None),
        P("dom", None, None),
        P(("group", "sub"), "dom"),
        P(None, ("group", "sub"), "dom"),
        P(("group", "sub"), "dom"),
        P(("group", "sub"), "dom", None),
        P(("group", "sub"), "dom", None, None, None),
    )
    return jax.shard_map(
        body,
        mesh=mesh,
        in_specs=placed,
        out_specs=(P("dom", None, ("group", "sub"), None, None), P(("group", "sub"), "dom")),
        check_vma=False,
    )
```
